32 devices in a mesh: grp: 2 (over x), par: 8 (over z, y), ex: 2 (over core).
Axes of the slice: x: 2, y: 2, z: 4, core: 2. Of those that a mesh axis runs over, the one named last changes fastest.
Arguments:
- gradients: bfloat16 [512, 16384], P(('grp', 'ex'), 'par'), parts along dimension 0
- proj_seed: int32 [1], replicated, may hold values from 0 to 999999
- block_keys: int32 [1, 32], P(None, 'par'), may hold values from 0 to 999999
Outputs:
- features: bfloat16 [512, 8192], P(('grp', 'ex'), 'par'), parts along dimension 0
- kernel: float32 [512, 256], P(('grp', 'par'), 'ex'), parts along dimension 0
The draws below stay inside these ranges and needn't reach their ends.
There are 2 independent parts, one for each index of `grp`. The reference program is written for one: setup_inputs(seed, part) draws one part's arguments, and reference() takes and returns one part's arrays. A program takes and returns all parts, laid end to end along the dimension named above; an argument that names none is the same for every part. Nothing has to cross between parts.
All inputs are finite; a program needn't handle non-finite values.
Results may differ from the reference program's by a relative error of at most 0.01.
Values may be sent and summed in bfloat16 or wider, within the bound.
A program may use at most 64 MiB of HBM per device.

```python
import math
import jax
import jax.numpy as jnp
from jax import lax

K = 8192
PBLK = 512
P_DEV = 2048
P_SIZE = 16384
EXAMPLES = 256
NBLK = 32
N_PAR = 8


def draw_gradients(key, part):
    first, second, third = jax.random.split(key, 3)
    row_scale = jnp.exp(jax.random.uniform(first, (EXAMPLES, 1), jnp.float32, math.log(0.2), math.log(2.0)))
    col_scale = jnp.exp(jax.random.uniform(second, (1, P_SIZE), jnp.float32, math.log(0.3), math.log(3.0)))
    noise = jax.random.normal(third, (EXAMPLES, P_SIZE), jnp.float32)
    values = noise * row_scale * col_scale
    return values.astype(jnp.bfloat16)


def place_ends(values, key, least, high):
    place = [jax.random.randint(jax.random.fold_in(key, axis), (), 0, length) for axis, length in enumerate(values.shape)]
    longest = values.shape.index(max(values.shape))
    beside = place[:longest] + [(place[longest] + 1) % values.shape[longest]] + place[longest + 1:]
    return values.at[tuple(place)].set(least).at[tuple(beside)].set(high)


def setup_inputs(seed: int = 0, part: int = 0) -> dict:
    arg_keys = jax.random.split(jax.random.key(seed), 4)
    part_keys = jax.random.split(jax.random.fold_in(arg_keys[3], part), 4)
    gradients = draw_gradients(jax.random.fold_in(jax.random.fold_in(arg_keys[3], part), 71), part)
    proj_seed = jax.random.randint(arg_keys[1], (1,), 0, 1000000).astype(jnp.int32)
    block_keys = place_ends(jax.random.randint(arg_keys[2], (1, NBLK), 0, 1000000), jax.random.fold_in(arg_keys[2], 1), 0, 999999).astype(jnp.int32)
    return dict(gradients=gradients, proj_seed=proj_seed, block_keys=block_keys)


def rademacher(seed_value, block_key, row_index, col_index):
    mixed = row_index * 73856093 ^ col_index * 19349663 ^ block_key * 83492791 ^ seed_value
    mixed = mixed ^ mixed >> 13 & 524287
    mixed = mixed * 1540483477
    mixed = mixed ^ mixed >> 15 & 131071
    parity = mixed >> 11 & 1
    return (1 - 2 * parity).astype(jnp.bfloat16)

def reference(gradients, proj_seed, block_keys):
    examples = gradients.shape[0]
    block_count = P_DEV // PBLK
    seed_value = proj_seed[0]
    key_row = block_keys[0]
    local_rows = jnp.arange(PBLK, dtype=jnp.int32)[:, None]
    col_index = jnp.arange(K, dtype=jnp.int32)[None, :]

    def shard_step(summed, shard):

        def block_step(partial_value, number):
            base = (shard * P_DEV + number * PBLK).astype(jnp.int32)
            slab_part = lax.dynamic_slice_in_dim(gradients, base, PBLK, 1).astype(jnp.float32)
            block_key = lax.dynamic_slice_in_dim(key_row, (shard * block_count + number).astype(jnp.int32), 1)[0]
            sign_block = rademacher(seed_value, block_key, local_rows + base, col_index).astype(jnp.float32)
            return (partial_value + jnp.dot(slab_part, sign_block, precision=lax.Precision.HIGHEST), None)
        partial_value, _ = lax.scan(block_step, jnp.zeros((examples, K), jnp.float32), jnp.arange(block_count, dtype=jnp.int32))
        rounded = lax.optimization_barrier(partial_value.astype(jnp.bfloat16)).astype(jnp.float32)
        return (summed + rounded, None)
    projected, _ = lax.scan(shard_step, jnp.zeros((examples, K), jnp.float32), jnp.arange(N_PAR, dtype=jnp.int32))
    features = jnp.tanh(projected * (1.0 / math.sqrt(P_SIZE))).astype(jnp.bfloat16)
    kernel = jnp.dot(features, features.T, preferred_element_type=jnp.float32) * (1.0 / math.sqrt(K))
    return (features, kernel)
```

```python
import functools
import math

import jax
import jax.numpy as jnp
import numpy as np
from jax import lax
from jax.experimental import pallas as pl
from jax.experimental.pallas import tpu as pltpu
from jax.sharding import PartitionSpec as P

K = 8192
PBLK = 512
MESH = pl.DeviceIdType.MESH
ROW_MUL = 73856093
COL_MUL = 19349663
KEY_MUL = 83492791
MIX_MUL = int(np.array((1540483477 << 5) & 0xFFFFFFFF, np.uint32).astype(np.int32))

NC = 2
STEPS = 4


def rademacher(seed_value, block_key, row_index, col_index):
    mixed = row_index * 73856093 ^ col_index * 19349663 ^ block_key * 83492791 ^ seed_value
    mixed = mixed ^ mixed >> 13 & 524287
    mixed = mixed * 1540483477
    mixed = mixed ^ mixed >> 15 & 131071
    parity = mixed >> 11 & 1
    return (1 - 2 * parity).astype(jnp.bfloat16)


def project(slab, key_row, row_base, seed_value, col_index):
    block_count = slab.shape[1] // PBLK
    local_rows = jnp.arange(PBLK, dtype=jnp.int32)[:, None]
    summed = None
    for number in range(block_count):
        sign_block = rademacher(
            seed_value, key_row[number], row_base + number * PBLK + local_rows, col_index
        )
        slab_part = slab[:, number * PBLK : (number + 1) * PBLK]
        product = jnp.dot(slab_part, sign_block, preferred_element_type=jnp.float32)
        summed = product if summed is None else summed + product
    return summed


def general(gradients, proj_seed, block_keys):
    local_params = gradients.shape[1]
    shard_count = lax.axis_size("par")
    shard_index = lax.axis_index("par")
    seed_value = proj_seed[0]
    all_cols = jnp.arange(K, dtype=jnp.int32)[None, :]
    partial_value = project(
        gradients, block_keys[0], shard_index * local_params, seed_value, all_cols
    )
    projected = lax.psum_scatter(
        partial_value.astype(jnp.bfloat16), "par", scatter_dimension=1, tiled=True
    ).astype(jnp.float32)
    features = jnp.tanh(projected * (1.0 / math.sqrt(local_params * shard_count))).astype(
        jnp.bfloat16
    )
    gathered = lax.all_gather(features, "ex", axis=0, tiled=True)
    product = lax.dot_general(
        gathered, features, (((1,), (1,)), ((), ())), preferred_element_type=jnp.float32
    )
    kernel = lax.psum_scatter(
        (product * (1.0 / math.sqrt(K))).astype(jnp.bfloat16),
        "par",
        scatter_dimension=0,
        tiled=True,
    ).astype(jnp.float32)
    return (features, kernel)


def fold(value):
    return value ^ lax.shift_right_logical(value, 13)


def line_kernel(
    seed_ref, key_ref, g_ref, feat_ref, kern_ref,
    x, signs, rows, keys, acc, outbox, inbox, feats, feats_in, kout, kin,
    y_send, y_recv, c_send, c_recv, f_send, f_recv, key_sems,
    z_send, z_recv, fx_send, fx_recv, k_send, k_recv,
):
    ex_rows, params = g_ref.shape
    chunk = ex_rows // NC
    width = K // 16
    par, ex = lax.axis_index("par"), lax.axis_index("ex")
    z, y = par // 2, par % 2
    other_y, other_ex = 1 - y, 1 - ex
    side = z // 2
    is_end = jnp.logical_or(z == 0, z == 3)
    is_mid = jnp.logical_not(is_end)
    me = par * 2 + ex
    blocks = params // PBLK

    barrier = pltpu.get_barrier_semaphore()

    def at_offset(k):
        target = lax.rem(me + k, 16)
        return {"par": target // 2, "ex": target % 2}

    for k in range(1, 16):
        pl.semaphore_signal(barrier, inc=1, device_id=at_offset(k), device_id_type=MESH)
    pl.semaphore_wait(barrier, 15)

    def remote(src, dst, send, recv, device):
        return pltpu.make_async_remote_copy(
            src_ref=src, dst_ref=dst, send_sem=send, recv_sem=recv,
            device_id=device, device_id_type=MESH,
        )

    y_dev = {"par": z * 2 + other_y}
    c_dev = {"ex": other_ex}
    for b in range(blocks):
        keys[y, b : b + 1, :] = jnp.full((1, 128), key_ref[0, b], jnp.int32)
    key_copy = remote(keys.at[y], keys.at[y], key_sems.at[0], key_sems.at[1], y_dev)
    key_copy.start()
    y_copies, c_copies, f_copies = [], [], []
    for c in range(NC):
        part = g_ref.at[pl.ds(c * chunk, chunk)]
        y_copies.append(remote(part, x.at[c, y, ex], y_send.at[c], y_recv.at[c], y_dev))
        c_copies.append(remote(part, x.at[c, y, ex], c_send.at[c], c_recv.at[c], c_dev))
        f_copies.append(
            remote(
                x.at[c, other_y, ex], x.at[c, other_y, ex], f_send.at[c], f_recv.at[c], c_dev
            )
        )
        y_copies[c].start()
    for c in range(NC):
        c_copies[c].start()
        x[c, y, ex] = g_ref[c * chunk : (c + 1) * chunk]

    seed = seed_ref[0]

    def make_rows(half):
        for b in range(blocks):
            index = lax.broadcasted_iota(jnp.int32, (PBLK, 128), 0)
            index = index + ((z * 2 + half) * params + b * PBLK)
            value = index * ROW_MUL ^ (keys[half, b : b + 1, :] * KEY_MUL ^ seed)
            rows[half, b * PBLK : (b + 1) * PBLK, :] = fold(value)

    def dest(step):
        near = jnp.where(side == 0, z, 3 - z)
        order = (3, 2, jnp.where(near == 0, 1, 0), near)[step]
        return jnp.where(side == 0, order, 3 - order)

    TILE = 64

    def make_signs(step, half):
        base = (dest(step) * 2 + y) * (2 * width) + ex * width
        cols = []
        for j in range(width // 128):
            col = lax.broadcasted_iota(jnp.int32, (8, 128), 1) + (base + j * 128)
            cols.append(fold(col * COL_MUL)[:1])

        def body(i, carry):
            start = pl.multiple_of(i * TILE, TILE)
            row = rows[half, pl.ds(start, TILE), :]
            for j, col in enumerate(cols):
                mixed = (row ^ col) * MIX_MUL
                mixed = mixed ^ (mixed << 15)
                sign = jnp.where(mixed < 0, -1.0, 1.0).astype(jnp.bfloat16)
                signs[step, half, pl.ds(start, TILE), j * 128 : (j + 1) * 128] = sign
            return carry

        lax.fori_loop(0, params // TILE, body, 0)

    end_dev = {"par": (1 + side) * 2 + y}
    far_dev = {"par": (3 - z) * 2 + y}
    near_dev = {"par": (3 * side) * 2 + y}

    def end_copy(c, s):
        return remote(outbox.at[c, s], inbox.at[s, c], z_send.at[c, s], z_recv.at[s, c], end_dev)

    def mid_copy(c, s):
        slot = 3 + s
        return remote(
            outbox.at[c, s], inbox.at[slot, c], z_send.at[c, s], z_recv.at[slot, c],
            far_dev if s < 2 else near_dev,
        )

    def arrived(slot, c):
        remote(
            inbox.at[slot, c], inbox.at[slot, c], z_send.at[c, 0], z_recv.at[slot, c], end_dev
        ).wait_recv()

    def multiply(c, s):
        for n in range(width // 256):
            cols = slice(n * 256, (n + 1) * 256)
            total = None
            for half in range(2):
                left = x[c, half].reshape(2 * chunk, params)
                product = jnp.dot(
                    left, signs[s, half, :, cols], preferred_element_type=jnp.float32
                )
                total = product if total is None else total + product
            acc[c, s, :, cols] = total
        if s < 3:

            @pl.when(is_end)
            def _():
                outbox[c, s] = acc[c, s].astype(jnp.bfloat16)
                end_copy(c, s).start()

    def finish(c, s):
        @pl.when(is_mid)
        def _():
            slot = (0, 1, 3)[s]
            arrived(slot, c)
            outbox[c, s] = (acc[c, s] + inbox[slot, c].astype(jnp.float32)).astype(jnp.bfloat16)
            mid_copy(c, s).start()

    scale = 1.0 / math.sqrt(params * 8)

    def fx_copy(c):
        return remote(
            feats.at[other_ex, pl.ds(c * chunk, chunk)], feats_in.at[pl.ds(c * chunk, chunk)],
            fx_send.at[c], fx_recv.at[c], c_dev,
        )

    def settle(c):
        @pl.when(is_mid)
        def _():
            arrived(2, c)
            arrived(4, c)
            acc[c, 3] += inbox[2, c].astype(jnp.float32) + inbox[4, c].astype(jnp.float32)

        @pl.when(is_end)
        def _():
            arrived(5, c)
            acc[c, 3] += inbox[5, c].astype(jnp.float32)

        value = jnp.tanh(acc[c, 3] * scale).astype(jnp.bfloat16)
        feats[:, c * chunk : (c + 1) * chunk, :] = value.reshape(2, chunk, width)
        fx_copy(c).start()

    def gathered(c):
        c_copies[c].wait_recv()
        f_copies[c].wait_recv()

    make_rows(y)
    make_signs(0, y)
    key_copy.wait_recv()
    make_rows(other_y)
    make_signs(0, other_y)
    y_copies[0].wait_recv()
    f_copies[0].start()
    gathered(0)
    multiply(0, 0)
    for s in (1, 2):
        for half in range(2):
            make_signs(s, half)
        finish(0, s - 1)
        multiply(0, s)
    y_copies[1].wait_recv()
    f_copies[1].start()
    for half in range(2):
        make_signs(3, half)
    finish(0, 2)
    gathered(1)
    multiply(1, 0)
    multiply(1, 1)
    finish(1, 0)
    multiply(1, 2)
    finish(1, 1)
    multiply(0, 3)
    finish(1, 2)
    settle(0)
    multiply(1, 3)
    settle(1)

    whole = feats[...].reshape(2 * ex_rows, width)
    product = lax.dot_general(
        whole, whole, (((1,), (1,)), ((), ())), preferred_element_type=jnp.float32
    ) * (1.0 / math.sqrt(K))
    for half in range(2):
        columns = product[:, half * 128 : (half + 1) * 128].astype(jnp.bfloat16)
        kout[half] = columns.reshape(8, 32, 128)

    def k_copy(k):
        target = lax.rem(me + k, 16)
        return remote(
            kout.at[target % 2, target // 2], kin.at[k], k_send.at[k], k_recv.at[k], at_offset(k)
        )

    for k in range(1, 16):
        k_copy(k).start()
    feat_ref[:, pl.ds(pl.multiple_of(ex * width, width), width)] = feats[ex]
    for c in range(NC):
        fx_copy(c).wait_recv()
    feat_ref[:, pl.ds(pl.multiple_of(other_ex * width, width), width)] = feats_in[...]
    total = kout[ex, par].astype(jnp.float32)
    for k in range(1, 16):
        k_copy(k).wait_recv()
        total += kin[k].astype(jnp.float32)
    kern_ref[...] = total

    key_copy.wait_send()
    for c in range(NC):
        y_copies[c].wait_send()
        c_copies[c].wait_send()
        f_copies[c].wait_send()
        fx_copy(c).wait_send()
        for s in range(3):
            end_copy(c, s).wait_send()
    for k in range(1, 16):
        k_copy(k).wait_send()


def line(gradients, proj_seed, block_keys):
    ex_rows, params = gradients.shape
    chunk = ex_rows // NC
    width = K // 16
    dma = pltpu.SemaphoreType.DMA
    bf16 = jnp.bfloat16
    return pl.pallas_call(
        line_kernel,
        out_shape=(
            jax.ShapeDtypeStruct((ex_rows, K // 8), bf16),
            jax.ShapeDtypeStruct((2 * ex_rows // 8, ex_rows), jnp.float32),
        ),
        in_specs=[
            pl.BlockSpec(memory_space=pltpu.SMEM),
            pl.BlockSpec(memory_space=pltpu.SMEM),
            pl.BlockSpec(memory_space=pltpu.VMEM),
        ],
        out_specs=(
            pl.BlockSpec(memory_space=pltpu.VMEM),
            pl.BlockSpec(memory_space=pltpu.VMEM),
        ),
        scratch_shapes=[
            pltpu.VMEM((NC, 2, 2, chunk, params), bf16),
            pltpu.VMEM((STEPS, 2, params, width), bf16),
            pltpu.VMEM((2, params, 128), jnp.int32),
            pltpu.VMEM((2, 8, 128), jnp.int32),
            pltpu.VMEM((NC, STEPS, 2 * chunk, width), jnp.float32),
            pltpu.VMEM((NC, 3, 2 * chunk, width), bf16),
            pltpu.VMEM((6, NC, 2 * chunk, width), bf16),
            pltpu.VMEM((2, ex_rows, width), bf16),
            pltpu.VMEM((ex_rows, width), bf16),
            pltpu.VMEM((2, 8, 32, 128), bf16),
            pltpu.VMEM((16, 32, 128), bf16),
            dma((NC,)), dma((NC,)), dma((NC,)), dma((NC,)), dma((NC,)), dma((NC,)),
            dma((2,)),
            dma((NC, 3)), dma((6, NC)), dma((NC,)), dma((NC,)), dma((16,)), dma((16,)),
        ],
        compiler_params=pltpu.CompilerParams(
            collective_id=0, has_side_effects=True, vmem_limit_bytes=56 * 1024 * 1024
        ),
    )(proj_seed, block_keys, gradients)


def solution(mesh):
    placed = (P(("grp", "ex"), "par"), P(), P(None, "par"))
    special = mesh.shape["par"] == 8 and mesh.shape["ex"] == 2
    return jax.shard_map(
        line if special else general,
        mesh=mesh,
        in_specs=placed,
        out_specs=(P(("grp", "ex"), "par"), P(("grp", "par"), "ex")),
        check_vma=False,
    )
```

```python
import functools
import math

import jax
import jax.numpy as jnp
import numpy as np
from jax import lax
from jax.experimental import pallas as pl
from jax.experimental.pallas import tpu as pltpu
from jax.sharding import PartitionSpec as P

K = 8192
PBLK = 512
MESH = pl.DeviceIdType.MESH
ROW_MUL = 73856093
COL_MUL = 19349663
KEY_MUL = 83492791
MIX_MUL = int(np.array((1540483477 << 5) & 0xFFFFFFFF, np.uint32).astype(np.int32))

NC = 4
STEPS = 4


def rademacher(seed_value, block_key, row_index, col_index):
    mixed = row_index * 73856093 ^ col_index * 19349663 ^ block_key * 83492791 ^ seed_value
    mixed = mixed ^ mixed >> 13 & 524287
    mixed = mixed * 1540483477
    mixed = mixed ^ mixed >> 15 & 131071
    parity = mixed >> 11 & 1
    return (1 - 2 * parity).astype(jnp.bfloat16)


def project(slab, key_row, row_base, seed_value, col_index):
    block_count = slab.shape[1] // PBLK
    local_rows = jnp.arange(PBLK, dtype=jnp.int32)[:, None]
    summed = None
    for number in range(block_count):
        sign_block = rademacher(
            seed_value, key_row[number], row_base + number * PBLK + local_rows, col_index
        )
        slab_part = slab[:, number * PBLK : (number + 1) * PBLK]
        product = jnp.dot(slab_part, sign_block, preferred_element_type=jnp.float32)
        summed = product if summed is None else summed + product
    return summed


def general(gradients, proj_seed, block_keys):
    local_params = gradients.shape[1]
    shard_count = lax.axis_size("par")
    shard_index = lax.axis_index("par")
    seed_value = proj_seed[0]
    all_cols = jnp.arange(K, dtype=jnp.int32)[None, :]
    partial_value = project(
        gradients, block_keys[0], shard_index * local_params, seed_value, all_cols
    )
    projected = lax.psum_scatter(
        partial_value.astype(jnp.bfloat16), "par", scatter_dimension=1, tiled=True
    ).astype(jnp.float32)
    features = jnp.tanh(projected * (1.0 / math.sqrt(local_params * shard_count))).astype(
        jnp.bfloat16
    )
    gathered = lax.all_gather(features, "ex", axis=0, tiled=True)
    product = lax.dot_general(
        gathered, features, (((1,), (1,)), ((), ())), preferred_element_type=jnp.float32
    )
    kernel = lax.psum_scatter(
        (product * (1.0 / math.sqrt(K))).astype(jnp.bfloat16),
        "par",
        scatter_dimension=0,
        tiled=True,
    ).astype(jnp.float32)
    return (features, kernel)


def fold(value):
    return value ^ lax.shift_right_logical(value, 13)


def line_kernel(
    seed_ref, key_ref, g_ref, feat_ref, kern_ref,
    x, signs, rows, keys, acc, outbox, inbox, feats, feats_in, kout, kin,
    y_send, y_recv, c_send, c_recv, f_send, f_recv, key_sems,
    z_send, z_recv, fx_send, fx_recv, k_send, k_recv,
):
    ex_rows, params = g_ref.shape
    chunk = ex_rows // NC
    width = K // 16
    par, ex = lax.axis_index("par"), lax.axis_index("ex")
    z, y = par // 2, par % 2
    other_y, other_ex = 1 - y, 1 - ex
    side = z // 2
    is_end = jnp.logical_or(z == 0, z == 3)
    is_mid = jnp.logical_not(is_end)
    me = par * 2 + ex
    blocks = params // PBLK

    barrier = pltpu.get_barrier_semaphore()

    def at_offset(k):
        target = lax.rem(me + k, 16)
        return {"par": target // 2, "ex": target % 2}

    for k in range(1, 16):
        pl.semaphore_signal(barrier, inc=1, device_id=at_offset(k), device_id_type=MESH)

    def remote(src, dst, send, recv, device):
        return pltpu.make_async_remote_copy(
            src_ref=src, dst_ref=dst, send_sem=send, recv_sem=recv,
            device_id=device, device_id_type=MESH,
        )

    y_dev = {"par": z * 2 + other_y}
    c_dev = {"ex": other_ex}
    for b in range(blocks):
        keys[y, b : b + 1, :] = jnp.full((1, 128), key_ref[0, b], jnp.int32)
    seed = seed_ref[0]

    def make_rows(half):
        for b in range(blocks):
            index = lax.broadcasted_iota(jnp.int32, (PBLK, 128), 0)
            index = index + ((z * 2 + half) * params + b * PBLK)
            value = index * ROW_MUL ^ (keys[half, b : b + 1, :] * KEY_MUL ^ seed)
            rows[half, b * PBLK : (b + 1) * PBLK, :] = fold(value)

    def dest(step):
        near = jnp.where(side == 0, z, 3 - z)
        order = (3, 2, jnp.where(near == 0, 1, 0), near)[step]
        return jnp.where(side == 0, order, 3 - order)

    TILE = 64

    def make_signs(step, half):
        base = (dest(step) * 2 + y) * (2 * width) + ex * width
        cols = []
        for j in range(width // 128):
            col = lax.broadcasted_iota(jnp.int32, (8, 128), 1) + (base + j * 128)
            cols.append(fold(col * COL_MUL)[:1])

        def body(i, carry):
            start = pl.multiple_of(i * TILE, TILE)
            row = rows[half, pl.ds(start, TILE), :]
            for j, col in enumerate(cols):
                mixed = (row ^ col) * MIX_MUL
                mixed = mixed ^ (mixed << 15)
                sign = jnp.where(mixed < 0, -1.0, 1.0).astype(jnp.bfloat16)
                signs[step, half, pl.ds(start, TILE), j * 128 : (j + 1) * 128] = sign
            return carry

        lax.fori_loop(0, params // TILE, body, 0)

    end_dev = {"par": (1 + side) * 2 + y}
    far_dev = {"par": (3 - z) * 2 + y}
    near_dev = {"par": (3 * side) * 2 + y}

    def end_copy(c, s):
        return remote(outbox.at[c, s], inbox.at[s, c], z_send.at[c, s], z_recv.at[s, c], end_dev)

    def mid_copy(c, s):
        slot = 3 + s
        return remote(
            outbox.at[c, s], inbox.at[slot, c], z_send.at[c, s], z_recv.at[slot, c],
            far_dev if s < 2 else near_dev,
        )

    def arrived(slot, c):
        remote(
            inbox.at[slot, c], inbox.at[slot, c], z_send.at[c, 0], z_recv.at[slot, c], end_dev
        ).wait_recv()

    def multiply_own(s):
        left = x[y].reshape(2 * ex_rows, params)
        for n in range(width // 256):
            cols = slice(n * 256, (n + 1) * 256)
            product = jnp.dot(left, signs[s, y, :, cols], preferred_element_type=jnp.float32)
            acc[s, :, :, cols] = product.reshape(NC, 2 * chunk, 256)

    def multiply(first, count, s):
        left = x[other_y, first : first + count].reshape(count * 2 * chunk, params)
        for n in range(width // 256):
            cols = slice(n * 256, (n + 1) * 256)
            product = jnp.dot(
                left, signs[s, other_y, :, cols], preferred_element_type=jnp.float32
            )
            acc[s, first : first + count, :, cols] += product.reshape(count, 2 * chunk, 256)
        if s < 3:

            @pl.when(is_end)
            def _():
                for c in range(first, first + count):
                    outbox[c, s] = acc[s, c].astype(jnp.bfloat16)
                    end_copy(c, s).start()

    def finish(c, s):
        @pl.when(is_mid)
        def _():
            slot = (0, 1, 3)[s]
            arrived(slot, c)
            outbox[c, s] = (acc[s, c] + inbox[slot, c].astype(jnp.float32)).astype(jnp.bfloat16)
            mid_copy(c, s).start()

    scale = 1.0 / math.sqrt(params * 8)

    def fx_copy(c):
        return remote(
            feats.at[other_ex, pl.ds(c * chunk, chunk)], feats_in.at[pl.ds(c * chunk, chunk)],
            fx_send.at[c], fx_recv.at[c], c_dev,
        )

    def settle(c):
        @pl.when(is_mid)
        def _():
            arrived(2, c)
            arrived(4, c)
            acc[3, c] += inbox[2, c].astype(jnp.float32) + inbox[4, c].astype(jnp.float32)

        @pl.when(is_end)
        def _():
            arrived(5, c)
            acc[3, c] += inbox[5, c].astype(jnp.float32)

        value = jnp.tanh(acc[3, c] * scale).astype(jnp.bfloat16)
        feats[:, c * chunk : (c + 1) * chunk, :] = value.reshape(2, chunk, width)
        fx_copy(c).start()

    def forward(c):
        y_copies[c].wait_recv()
        f_copies[c].start()

    make_rows(y)
    for step in range(3):
        make_signs(step, y)
    for c in range(NC):
        x[y, c, ex] = g_ref[c * chunk : (c + 1) * chunk]
    pl.semaphore_wait(barrier, 15)

    key_copy = remote(keys.at[y], keys.at[y], key_sems.at[0], key_sems.at[1], y_dev)
    key_copy.start()
    y_copies, c_copies, f_copies = [], [], []
    for c in range(NC):
        part = g_ref.at[pl.ds(c * chunk, chunk)]
        y_copies.append(remote(part, x.at[y, c, ex], y_send.at[c], y_recv.at[c], y_dev))
        c_copies.append(remote(part, x.at[y, c, ex], c_send.at[c], c_recv.at[c], c_dev))
        f_copies.append(
            remote(
                x.at[other_y, c, ex], x.at[other_y, c, ex], f_send.at[c], f_recv.at[c], c_dev
            )
        )
        y_copies[c].start()
    for c in range(NC):
        c_copies[c].start()

    make_signs(3, y)
    key_copy.wait_recv()
    make_rows(other_y)
    make_signs(0, other_y)
    for c in range(NC):
        c_copies[c].wait_recv()
    multiply_own(0)
    multiply_own(1)
    forward(0)
    make_signs(1, other_y)
    f_copies[0].wait_recv()
    multiply(0, 1, 0)
    multiply(0, 1, 1)
    forward(1)
    make_signs(2, other_y)
    f_copies[1].wait_recv()
    multiply(1, 1, 0)
    multiply(1, 1, 1)
    finish(0, 0)
    finish(0, 1)
    forward(2)
    multiply_own(2)
    f_copies[2].wait_recv()
    multiply(2, 1, 0)
    multiply(2, 1, 1)
    finish(1, 0)
    finish(1, 1)
    forward(3)
    make_signs(3, other_y)
    f_copies[3].wait_recv()
    multiply(3, 1, 0)
    multiply(3, 1, 1)
    multiply(0, 2, 2)
    finish(2, 0)
    finish(2, 1)
    finish(0, 2)
    multiply(2, 2, 2)
    finish(3, 0)
    finish(3, 1)
    finish(1, 2)
    finish(2, 2)
    multiply_own(3)
    multiply(0, NC, 3)
    finish(3, 2)
    for c in range(NC):
        settle(c)

    whole = feats[...].reshape(2 * ex_rows, width)
    product = lax.dot_general(
        whole, whole, (((1,), (1,)), ((), ())), preferred_element_type=jnp.float32
    ) * (1.0 / math.sqrt(K))
    for half in range(2):
        columns = product[:, half * 128 : (half + 1) * 128].astype(jnp.bfloat16)
        kout[half] = columns.reshape(8, 32, 128)

    def k_copy(k):
        target = lax.rem(me + k, 16)
        return remote(
            kout.at[target % 2, target // 2], kin.at[k], k_send.at[k], k_recv.at[k], at_offset(k)
        )

    for k in range(1, 16):
        k_copy(k).start()
    feat_ref[:, pl.ds(pl.multiple_of(ex * width, width), width)] = feats[ex]
    for c in range(NC):
        fx_copy(c).wait_recv()
    feat_ref[:, pl.ds(pl.multiple_of(other_ex * width, width), width)] = feats_in[...]
    total = kout[ex, par].astype(jnp.float32)
    for k in range(1, 16):
        k_copy(k).wait_recv()
        total += kin[k].astype(jnp.float32)
    kern_ref[...] = total

    key_copy.wait_send()
    for c in range(NC):
        y_copies[c].wait_send()
        c_copies[c].wait_send()
        f_copies[c].wait_send()
        fx_copy(c).wait_send()
        for s in range(3):
            end_copy(c, s).wait_send()
    for k in range(1, 16):
        k_copy(k).wait_send()


def write_kernel(feat_in, kern_in, feat_ref, kern_ref):
    feat_ref[...] = feat_in[...]
    kern_ref[...] = kern_in[...]


def line(gradients, proj_seed, block_keys):
    ex_rows, params = gradients.shape
    chunk = ex_rows // NC
    width = K // 16
    dma = pltpu.SemaphoreType.DMA
    bf16 = jnp.bfloat16
    pair = pl.pallas_call(
        line_kernel,
        out_shape=(
            jax.ShapeDtypeStruct((ex_rows, K // 8), bf16),
            jax.ShapeDtypeStruct((2 * ex_rows // 8, ex_rows), jnp.float32),
        ),
        in_specs=[
            pl.BlockSpec(memory_space=pltpu.SMEM),
            pl.BlockSpec(memory_space=pltpu.SMEM),
            pl.BlockSpec(memory_space=pltpu.VMEM),
        ],
        out_specs=(
            pl.BlockSpec(memory_space=pltpu.VMEM),
            pl.BlockSpec(memory_space=pltpu.VMEM),
        ),
        scratch_shapes=[
            pltpu.VMEM((2, NC, 2, chunk, params), bf16),
            pltpu.VMEM((STEPS, 2, params, width), bf16),
            pltpu.VMEM((2, params, 128), jnp.int32),
            pltpu.VMEM((2, 8, 128), jnp.int32),
            pltpu.VMEM((STEPS, NC, 2 * chunk, width), jnp.float32),
            pltpu.VMEM((NC, 3, 2 * chunk, width), bf16),
            pltpu.VMEM((6, NC, 2 * chunk, width), bf16),
            pltpu.VMEM((2, ex_rows, width), bf16),
            pltpu.VMEM((ex_rows, width), bf16),
            pltpu.VMEM((2, 8, 32, 128), bf16),
            pltpu.VMEM((16, 32, 128), bf16),
            dma((NC,)), dma((NC,)), dma((NC,)), dma((NC,)), dma((NC,)), dma((NC,)),
            dma((2,)),
            dma((NC, 3)), dma((6, NC)), dma((NC,)), dma((NC,)), dma((16,)), dma((16,)),
        ],
        compiler_params=pltpu.CompilerParams(
            collective_id=0, has_side_effects=True, vmem_limit_bytes=56 * 1024 * 1024
        ),
    )(proj_seed, block_keys, gradients)
    return pl.pallas_call(
        write_kernel,
        out_shape=tuple(jax.ShapeDtypeStruct(part.shape, part.dtype) for part in pair),
    )(*pair)


def solution(mesh):
    placed = (P(("grp", "ex"), "par"), P(), P(None, "par"))
    special = mesh.shape["par"] == 8 and mesh.shape["ex"] == 2
    return jax.shard_map(
        line if special else general,
        mesh=mesh,
        in_specs=placed,
        out_specs=(P(("grp", "ex"), "par"), P(("grp", "par"), "ex")),
        check_vma=False,
    )
```

```python
import functools
import math

import jax
import jax.numpy as jnp
import numpy as np
from jax import lax
from jax.experimental import pallas as pl
from jax.experimental.pallas import tpu as pltpu
from jax.sharding import PartitionSpec as P

K = 8192
PBLK = 512
MESH = pl.DeviceIdType.MESH
ROW_MUL = 73856093
COL_MUL = 19349663
KEY_MUL = 83492791
MIX_MUL = int(np.array((1540483477 << 5) & 0xFFFFFFFF, np.uint32).astype(np.int32))

NC = 4
STEPS = 4


def rademacher(seed_value, block_key, row_index, col_index):
    mixed = row_index * 73856093 ^ col_index * 19349663 ^ block_key * 83492791 ^ seed_value
    mixed = mixed ^ mixed >> 13 & 524287
    mixed = mixed * 1540483477
    mixed = mixed ^ mixed >> 15 & 131071
    parity = mixed >> 11 & 1
    return (1 - 2 * parity).astype(jnp.bfloat16)


def project(slab, key_row, row_base, seed_value, col_index):
    block_count = slab.shape[1] // PBLK
    local_rows = jnp.arange(PBLK, dtype=jnp.int32)[:, None]
    summed = None
    for number in range(block_count):
        sign_block = rademacher(
            seed_value, key_row[number], row_base + number * PBLK + local_rows, col_index
        )
        slab_part = slab[:, number * PBLK : (number + 1) * PBLK]
        product = jnp.dot(slab_part, sign_block, preferred_element_type=jnp.float32)
        summed = product if summed is None else summed + product
    return summed


def general(gradients, proj_seed, block_keys):
    local_params = gradients.shape[1]
    shard_count = lax.axis_size("par")
    shard_index = lax.axis_index("par")
    seed_value = proj_seed[0]
    all_cols = jnp.arange(K, dtype=jnp.int32)[None, :]
    partial_value = project(
        gradients, block_keys[0], shard_index * local_params, seed_value, all_cols
    )
    projected = lax.psum_scatter(
        partial_value.astype(jnp.bfloat16), "par", scatter_dimension=1, tiled=True
    ).astype(jnp.float32)
    features = jnp.tanh(projected * (1.0 / math.sqrt(local_params * shard_count))).astype(
        jnp.bfloat16
    )
    gathered = lax.all_gather(features, "ex", axis=0, tiled=True)
    product = lax.dot_general(
        gathered, features, (((1,), (1,)), ((), ())), preferred_element_type=jnp.float32
    )
    kernel = lax.psum_scatter(
        (product * (1.0 / math.sqrt(K))).astype(jnp.bfloat16),
        "par",
        scatter_dimension=0,
        tiled=True,
    ).astype(jnp.float32)
    return (features, kernel)


def fold(value):
    return value ^ lax.shift_right_logical(value, 13)


def line_kernel(
    seed_ref, key_ref, g_ref, feat_ref, kern_ref,
    x, signs, rows, keys, acc, outbox, inbox, feats, feats_in, kout, kin,
    y_send, y_recv, c_send, c_recv, f_send, f_recv, key_sems,
    z_send, z_recv, fx_send, fx_recv, k_send, k_recv,
):
    ex_rows, params = g_ref.shape
    chunk = ex_rows // NC
    width = K // 16
    par, ex = lax.axis_index("par"), lax.axis_index("ex")
    z, y = par // 2, par % 2
    other_y, other_ex = 1 - y, 1 - ex
    side = z // 2
    is_end = jnp.logical_or(z == 0, z == 3)
    is_mid = jnp.logical_not(is_end)
    me = par * 2 + ex
    blocks = params // PBLK

    barrier = pltpu.get_barrier_semaphore()

    def at_offset(k):
        target = lax.rem(me + k, 16)
        return {"par": target // 2, "ex": target % 2}

    y_dev = {"par": z * 2 + other_y}
    c_dev = {"ex": other_ex}
    end_dev = {"par": (1 + side) * 2 + y}
    far_dev = {"par": (3 - z) * 2 + y}
    near_dev = {"par": (3 * side) * 2 + y}
    pl.semaphore_signal(barrier, inc=1, device_id=y_dev, device_id_type=MESH)
    pl.semaphore_signal(barrier, inc=1, device_id=c_dev, device_id_type=MESH)

    @pl.when(is_end)
    def _():
        pl.semaphore_signal(barrier, inc=1, device_id=end_dev, device_id_type=MESH)

    @pl.when(is_mid)
    def _():
        pl.semaphore_signal(barrier, inc=1, device_id=far_dev, device_id_type=MESH)
        pl.semaphore_signal(barrier, inc=1, device_id=near_dev, device_id_type=MESH)

    def remote(src, dst, send, recv, device):
        return pltpu.make_async_remote_copy(
            src_ref=src, dst_ref=dst, send_sem=send, recv_sem=recv,
            device_id=device, device_id_type=MESH,
        )

    for b in range(blocks):
        keys[y, b : b + 1, :] = jnp.full((1, 128), key_ref[0, b], jnp.int32)
    seed = seed_ref[0]

    def make_rows(half):
        for b in range(blocks):
            index = lax.broadcasted_iota(jnp.int32, (PBLK, 128), 0)
            index = index + ((z * 2 + half) * params + b * PBLK)
            value = index * ROW_MUL ^ (keys[half, b : b + 1, :] * KEY_MUL ^ seed)
            rows[half, b * PBLK : (b + 1) * PBLK, :] = fold(value)

    def dest(step):
        near = jnp.where(side == 0, z, 3 - z)
        order = (3, 2, jnp.where(near == 0, 1, 0), near)[step]
        return jnp.where(side == 0, order, 3 - order)

    TILE = 64

    def make_signs(step, half):
        base = (dest(step) * 2 + y) * (2 * width) + ex * width
        cols = []
        for j in range(width // 128):
            col = lax.broadcasted_iota(jnp.int32, (8, 128), 1) + (base + j * 128)
            cols.append(fold(col * COL_MUL)[:1])

        def body(i, carry):
            start = pl.multiple_of(i * TILE, TILE)
            row = rows[half, pl.ds(start, TILE), :]
            for j, col in enumerate(cols):
                mixed = (row ^ col) * MIX_MUL
                mixed = mixed ^ (mixed << 15)
                sign = jnp.where(mixed < 0, -1.0, 1.0).astype(jnp.bfloat16)
                signs[step, half, pl.ds(start, TILE), j * 128 : (j + 1) * 128] = sign
            return carry

        lax.fori_loop(0, params // TILE, body, 0)

    def end_copy(c, s):
        return remote(outbox.at[c, s], inbox.at[s, c], z_send.at[c, s], z_recv.at[s, c], end_dev)

    def mid_copy(c, s):
        slot = 3 + s
        return remote(
            outbox.at[c, s], inbox.at[slot, c], z_send.at[c, s], z_recv.at[slot, c],
            far_dev if s < 2 else near_dev,
        )

    def arrived(slot, c):
        remote(
            inbox.at[slot, c], inbox.at[slot, c], z_send.at[c, 0], z_recv.at[slot, c], end_dev
        ).wait_recv()

    def multiply_own(s):
        left = x[y].reshape(2 * ex_rows, params)
        for n in range(width // 256):
            cols = slice(n * 256, (n + 1) * 256)
            product = jnp.dot(left, signs[s, y, :, cols], preferred_element_type=jnp.float32)
            acc[s, :, :, cols] = product.reshape(NC, 2 * chunk, 256)

    def multiply(first, count, s):
        left = x[other_y, first : first + count].reshape(count * 2 * chunk, params)
        for n in range(width // 256):
            cols = slice(n * 256, (n + 1) * 256)
            product = jnp.dot(
                left, signs[s, other_y, :, cols], preferred_element_type=jnp.float32
            )
            acc[s, first : first + count, :, cols] += product.reshape(count, 2 * chunk, 256)
        if s < 3:

            @pl.when(is_end)
            def _():
                for c in range(first, first + count):
                    outbox[c, s] = acc[s, c].astype(jnp.bfloat16)
                    end_copy(c, s).start()

    def finish(c, s):
        @pl.when(is_mid)
        def _():
            slot = (0, 1, 3)[s]
            arrived(slot, c)
            outbox[c, s] = (acc[s, c] + inbox[slot, c].astype(jnp.float32)).astype(jnp.bfloat16)
            mid_copy(c, s).start()

    scale = 1.0 / math.sqrt(params * 8)

    def fx_copy(c):
        return remote(
            feats.at[other_ex, pl.ds(c * chunk, chunk)], feats_in.at[pl.ds(c * chunk, chunk)],
            fx_send.at[c], fx_recv.at[c], c_dev,
        )

    def settle(c):
        @pl.when(is_mid)
        def _():
            arrived(2, c)
            arrived(4, c)
            acc[3, c] += inbox[2, c].astype(jnp.float32) + inbox[4, c].astype(jnp.float32)

        @pl.when(is_end)
        def _():
            arrived(5, c)
            acc[3, c] += inbox[5, c].astype(jnp.float32)

        value = jnp.tanh(acc[3, c] * scale).astype(jnp.bfloat16)
        feats[:, c * chunk : (c + 1) * chunk, :] = value.reshape(2, chunk, width)
        fx_copy(c).start()

    def forward(c):
        y_copies[c].wait_recv()
        f_copies[c].start()

    make_rows(y)
    for step in range(3):
        make_signs(step, y)
    for c in range(NC):
        x[y, c, ex] = g_ref[c * chunk : (c + 1) * chunk]

    @pl.when(is_end)
    def _():
        pl.semaphore_wait(barrier, 3)

    @pl.when(is_mid)
    def _():
        pl.semaphore_wait(barrier, 4)

    key_copy = remote(keys.at[y], keys.at[y], key_sems.at[0], key_sems.at[1], y_dev)
    key_copy.start()
    y_copies, c_copies, f_copies = [], [], []
    for c in range(NC):
        part = g_ref.at[pl.ds(c * chunk, chunk)]
        y_copies.append(remote(part, x.at[y, c, ex], y_send.at[c], y_recv.at[c], y_dev))
        c_copies.append(remote(part, x.at[y, c, ex], c_send.at[c], c_recv.at[c], c_dev))
        f_copies.append(
            remote(
                x.at[other_y, c, ex], x.at[other_y, c, ex], f_send.at[c], f_recv.at[c], c_dev
            )
        )
        y_copies[c].start()
    for c in range(NC):
        c_copies[c].start()

    make_signs(3, y)
    key_copy.wait_recv()
    make_rows(other_y)
    make_signs(0, other_y)
    for c in range(NC):
        c_copies[c].wait_recv()
    multiply_own(0)
    multiply_own(1)
    forward(0)
    make_signs(1, other_y)
    f_copies[0].wait_recv()
    multiply(0, 1, 0)
    multiply(0, 1, 1)
    forward(1)
    make_signs(2, other_y)
    f_copies[1].wait_recv()
    multiply(1, 1, 0)
    multiply(1, 1, 1)
    finish(0, 0)
    finish(0, 1)
    forward(2)
    multiply_own(2)
    f_copies[2].wait_recv()
    multiply(2, 1, 0)
    multiply(2, 1, 1)
    finish(1, 0)
    finish(1, 1)
    forward(3)
    make_signs(3, other_y)
    f_copies[3].wait_recv()
    multiply(3, 1, 0)
    multiply(3, 1, 1)
    multiply(0, 2, 2)
    finish(2, 0)
    finish(2, 1)
    finish(0, 2)
    multiply(2, 2, 2)
    finish(3, 0)
    finish(3, 1)
    finish(1, 2)
    multiply_own(3)
    finish(2, 2)
    multiply(0, NC, 3)
    settle(0)
    finish(3, 2)
    for c in range(1, NC):
        settle(c)

    whole = feats[...].reshape(2 * ex_rows, width)
    product = lax.dot_general(
        whole, whole, (((1,), (1,)), ((), ())), preferred_element_type=jnp.float32
    ) * (1.0 / math.sqrt(K))
    for half in range(2):
        columns = product[:, half * 128 : (half + 1) * 128].astype(jnp.bfloat16)
        kout[half] = columns.reshape(8, 32, 128)

    def k_copy(k):
        target = lax.rem(me + k, 16)
        return remote(
            kout.at[target % 2, target // 2], kin.at[k], k_send.at[k], k_recv.at[k], at_offset(k)
        )

    for k in range(1, 16):
        k_copy(k).start()
    feat_ref[:, pl.ds(pl.multiple_of(ex * width, width), width)] = feats[ex]
    for c in range(NC):
        fx_copy(c).wait_recv()
    feat_ref[:, pl.ds(pl.multiple_of(other_ex * width, width), width)] = feats_in[...]
    total = kout[ex, par].astype(jnp.float32)
    for k in range(1, 16):
        k_copy(k).wait_recv()
        total += kin[k].astype(jnp.float32)
    kern_ref[...] = total

    key_copy.wait_send()
    for c in range(NC):
        y_copies[c].wait_send()
        c_copies[c].wait_send()
        f_copies[c].wait_send()
        fx_copy(c).wait_send()
        for s in range(3):
            end_copy(c, s).wait_send()
    for k in range(1, 16):
        k_copy(k).wait_send()


def write_kernel(feat_in, kern_in, feat_ref, kern_ref):
    feat_ref[...] = feat_in[...]
    kern_ref[...] = kern_in[...]


def line(gradients, proj_seed, block_keys):
    ex_rows, params = gradients.shape
    chunk = ex_rows // NC
    width = K // 16
    dma = pltpu.SemaphoreType.DMA
    bf16 = jnp.bfloat16
    pair = pl.pallas_call(
        line_kernel,
        out_shape=(
            jax.ShapeDtypeStruct((ex_rows, K // 8), bf16),
            jax.ShapeDtypeStruct((2 * ex_rows // 8, ex_rows), jnp.float32),
        ),
        in_specs=[
            pl.BlockSpec(memory_space=pltpu.SMEM),
            pl.BlockSpec(memory_space=pltpu.SMEM),
            pl.BlockSpec(memory_space=pltpu.VMEM),
        ],
        out_specs=(
            pl.BlockSpec(memory_space=pltpu.VMEM),
            pl.BlockSpec(memory_space=pltpu.VMEM),
        ),
        scratch_shapes=[
            pltpu.VMEM((2, NC, 2, chunk, params), bf16),
            pltpu.VMEM((STEPS, 2, params, width), bf16),
            pltpu.VMEM((2, params, 128), jnp.int32),
            pltpu.VMEM((2, 8, 128), jnp.int32),
            pltpu.VMEM((STEPS, NC, 2 * chunk, width), jnp.float32),
            pltpu.VMEM((NC, 3, 2 * chunk, width), bf16),
            pltpu.VMEM((6, NC, 2 * chunk, width), bf16),
            pltpu.VMEM((2, ex_rows, width), bf16),
            pltpu.VMEM((ex_rows, width), bf16),
            pltpu.VMEM((2, 8, 32, 128), bf16),
            pltpu.VMEM((16, 32, 128), bf16),
            dma((NC,)), dma((NC,)), dma((NC,)), dma((NC,)), dma((NC,)), dma((NC,)),
            dma((2,)),
            dma((NC, 3)), dma((6, NC)), dma((NC,)), dma((NC,)), dma((16,)), dma((16,)),
        ],
        compiler_params=pltpu.CompilerParams(
            collective_id=0, has_side_effects=True, vmem_limit_bytes=56 * 1024 * 1024
        ),
    )(proj_seed, block_keys, gradients)
    return pl.pallas_call(
        write_kernel,
        out_shape=tuple(jax.ShapeDtypeStruct(part.shape, part.dtype) for part in pair),
    )(*pair)


def solution(mesh):
    placed = (P(("grp", "ex"), "par"), P(), P(None, "par"))
    special = mesh.shape["par"] == 8 and mesh.shape["ex"] == 2
    return jax.shard_map(
        line if special else general,
        mesh=mesh,
        in_specs=placed,
        out_specs=(P(("grp", "ex"), "par"), P(("grp", "par"), "ex")),
        check_vma=False,
    )
```

```python
import functools
import math

import jax
import jax.numpy as jnp
import numpy as np
from jax import lax
from jax.experimental import pallas as pl
from jax.experimental.pallas import tpu as pltpu
from jax.sharding import PartitionSpec as P

K = 8192
PBLK = 512
MESH = pl.DeviceIdType.MESH
ROW_MUL = 73856093
COL_MUL = 19349663
KEY_MUL = 83492791
MIX_MUL = int(np.array((1540483477 << 5) & 0xFFFFFFFF, np.uint32).astype(np.int32))

NC = 4
STEPS = 4


def rademacher(seed_value, block_key, row_index, col_index):
    mixed = row_index * 73856093 ^ col_index * 19349663 ^ block_key * 83492791 ^ seed_value
    mixed = mixed ^ mixed >> 13 & 524287
    mixed = mixed * 1540483477
    mixed = mixed ^ mixed >> 15 & 131071
    parity = mixed >> 11 & 1
    return (1 - 2 * parity).astype(jnp.bfloat16)


def project(slab, key_row, row_base, seed_value, col_index):
    block_count = slab.shape[1] // PBLK
    local_rows = jnp.arange(PBLK, dtype=jnp.int32)[:, None]
    summed = None
    for number in range(block_count):
        sign_block = rademacher(
            seed_value, key_row[number], row_base + number * PBLK + local_rows, col_index
        )
        slab_part = slab[:, number * PBLK : (number + 1) * PBLK]
        product = jnp.dot(slab_part, sign_block, preferred_element_type=jnp.float32)
        summed = product if summed is None else summed + product
    return summed


def general(gradients, proj_seed, block_keys):
    local_params = gradients.shape[1]
    shard_count = lax.axis_size("par")
    shard_index = lax.axis_index("par")
    seed_value = proj_seed[0]
    all_cols = jnp.arange(K, dtype=jnp.int32)[None, :]
    partial_value = project(
        gradients, block_keys[0], shard_index * local_params, seed_value, all_cols
    )
    projected = lax.psum_scatter(
        partial_value.astype(jnp.bfloat16), "par", scatter_dimension=1, tiled=True
    ).astype(jnp.float32)
    features = jnp.tanh(projected * (1.0 / math.sqrt(local_params * shard_count))).astype(
        jnp.bfloat16
    )
    gathered = lax.all_gather(features, "ex", axis=0, tiled=True)
    product = lax.dot_general(
        gathered, features, (((1,), (1,)), ((), ())), preferred_element_type=jnp.float32
    )
    kernel = lax.psum_scatter(
        (product * (1.0 / math.sqrt(K))).astype(jnp.bfloat16),
        "par",
        scatter_dimension=0,
        tiled=True,
    ).astype(jnp.float32)
    return (features, kernel)


def fold(value):
    return value ^ lax.shift_right_logical(value, 13)


def line_kernel(
    seed_ref, key_ref, g_ref, feat_ref, kern_ref,
    x, signs, rows, keys, acc, outbox, inbox, feats, feats_in, kout, kin,
    y_send, y_recv, c_send, c_recv, f_send, f_recv, key_sems,
    z_send, z_recv, fx_send, fx_recv, k_send, k_recv,
):
    ex_rows, params = g_ref.shape
    chunk = ex_rows // NC
    width = K // 16
    par, ex = lax.axis_index("par"), lax.axis_index("ex")
    z, y = par // 2, par % 2
    other_y, other_ex = 1 - y, 1 - ex
    side = z // 2
    is_end = jnp.logical_or(z == 0, z == 3)
    is_mid = jnp.logical_not(is_end)
    me = par * 2 + ex
    blocks = params // PBLK

    barrier = pltpu.get_barrier_semaphore()

    def at_offset(k):
        target = lax.rem(me + k, 16)
        return {"par": target // 2, "ex": target % 2}

    y_dev = {"par": z * 2 + other_y}
    c_dev = {"ex": other_ex}
    end_dev = {"par": (1 + side) * 2 + y}
    far_dev = {"par": (3 - z) * 2 + y}
    near_dev = {"par": (3 * side) * 2 + y}
    pl.semaphore_signal(barrier, inc=1, device_id=y_dev, device_id_type=MESH)
    pl.semaphore_signal(barrier, inc=1, device_id=c_dev, device_id_type=MESH)

    @pl.when(is_end)
    def _():
        pl.semaphore_signal(barrier, inc=1, device_id=end_dev, device_id_type=MESH)

    @pl.when(is_mid)
    def _():
        pl.semaphore_signal(barrier, inc=1, device_id=far_dev, device_id_type=MESH)
        pl.semaphore_signal(barrier, inc=1, device_id=near_dev, device_id_type=MESH)

    def remote(src, dst, send, recv, device):
        return pltpu.make_async_remote_copy(
            src_ref=src, dst_ref=dst, send_sem=send, recv_sem=recv,
            device_id=device, device_id_type=MESH,
        )

    for b in range(blocks):
        keys[y, b : b + 1, :] = jnp.full((1, 128), key_ref[0, b], jnp.int32)
    seed = seed_ref[0]

    def make_rows(half):
        for b in range(blocks):
            index = lax.broadcasted_iota(jnp.int32, (PBLK, 128), 0)
            index = index + ((z * 2 + half) * params + b * PBLK)
            value = index * ROW_MUL ^ (keys[half, b : b + 1, :] * KEY_MUL ^ seed)
            rows[half, b * PBLK : (b + 1) * PBLK, :] = fold(value)

    def dest(step):
        near = jnp.where(side == 0, z, 3 - z)
        order = (3, 2, jnp.where(near == 0, 1, 0), near)[step]
        return jnp.where(side == 0, order, 3 - order)

    TILE = 64

    def make_signs(step, half):
        base = (dest(step) * 2 + y) * (2 * width) + ex * width
        cols = []
        for j in range(width // 128):
            col = lax.broadcasted_iota(jnp.int32, (8, 128), 1) + (base + j * 128)
            cols.append(fold(col * COL_MUL)[:1])

        def body(i, carry):
            start = pl.multiple_of(i * TILE, TILE)
            row = rows[half, pl.ds(start, TILE), :]
            for j, col in enumerate(cols):
                mixed = (row ^ col) * MIX_MUL
                mixed = mixed ^ (mixed << 15)
                sign = jnp.where(mixed < 0, -1.0, 1.0).astype(jnp.bfloat16)
                signs[step, half, pl.ds(start, TILE), j * 128 : (j + 1) * 128] = sign
            return carry

        lax.fori_loop(0, params // TILE, body, 0)

    def end_copy(c, s):
        return remote(outbox.at[c, s], inbox.at[s, c], z_send.at[c, s], z_recv.at[s, c], end_dev)

    def mid_copy(c, s):
        slot = 3 + s
        return remote(
            outbox.at[c, s], inbox.at[slot, c], z_send.at[c, s], z_recv.at[slot, c],
            far_dev if s < 2 else near_dev,
        )

    def arrived(slot, c):
        remote(
            inbox.at[slot, c], inbox.at[slot, c], z_send.at[c, 0], z_recv.at[slot, c], end_dev
        ).wait_recv()

    def multiply_own(s):
        left = x[y].reshape(2 * ex_rows, params)
        for n in range(width // 256):
            cols = slice(n * 256, (n + 1) * 256)
            product = jnp.dot(left, signs[s, y, :, cols], preferred_element_type=jnp.float32)
            acc[s, :, :, cols] = product.reshape(NC, 2 * chunk, 256)

    def multiply(first, count, s):
        left = x[other_y, first : first + count].reshape(count * 2 * chunk, params)
        for n in range(width // 256):
            cols = slice(n * 256, (n + 1) * 256)
            product = jnp.dot(
                left, signs[s, other_y, :, cols], preferred_element_type=jnp.float32
            )
            acc[s, first : first + count, :, cols] += product.reshape(count, 2 * chunk, 256)
        if s < 3:

            @pl.when(is_end)
            def _():
                for c in range(first, first + count):
                    outbox[c, s] = acc[s, c].astype(jnp.bfloat16)
                    end_copy(c, s).start()

    def finish(c, s):
        @pl.when(is_mid)
        def _():
            slot = (0, 1, 3)[s]
            arrived(slot, c)
            outbox[c, s] = (acc[s, c] + inbox[slot, c].astype(jnp.float32)).astype(jnp.bfloat16)
            mid_copy(c, s).start()

    scale = 1.0 / math.sqrt(params * 8)

    def fx_copy(c):
        return remote(
            feats.at[other_ex, pl.ds(c * chunk, chunk)], feats_in.at[pl.ds(c * chunk, chunk)],
            fx_send.at[c], fx_recv.at[c], c_dev,
        )

    def settle(c):
        @pl.when(is_mid)
        def _():
            arrived(2, c)
            arrived(4, c)
            acc[3, c] += inbox[2, c].astype(jnp.float32) + inbox[4, c].astype(jnp.float32)

        @pl.when(is_end)
        def _():
            arrived(5, c)
            acc[3, c] += inbox[5, c].astype(jnp.float32)

        value = jnp.tanh(acc[3, c] * scale).astype(jnp.bfloat16)
        feats[:, c * chunk : (c + 1) * chunk, :] = value.reshape(2, chunk, width)
        fx_copy(c).start()

    def forward(c):
        y_copies[c].wait_recv()
        f_copies[c].start()

    @pl.when(is_end)
    def _():
        pl.semaphore_wait(barrier, 3)

    @pl.when(is_mid)
    def _():
        pl.semaphore_wait(barrier, 4)

    key_copy = remote(keys.at[y], keys.at[y], key_sems.at[0], key_sems.at[1], y_dev)
    key_copy.start()
    y_copies, c_copies, f_copies = [], [], []
    for c in range(NC):
        part = g_ref.at[pl.ds(c * chunk, chunk)]
        y_copies.append(remote(part, x.at[y, c, ex], y_send.at[c], y_recv.at[c], y_dev))
        c_copies.append(remote(part, x.at[y, c, ex], c_send.at[c], c_recv.at[c], c_dev))
        f_copies.append(
            remote(
                x.at[other_y, c, ex], x.at[other_y, c, ex], f_send.at[c], f_recv.at[c], c_dev
            )
        )
        y_copies[c].start()
    for c in range(NC):
        c_copies[c].start()

    for c in range(NC):
        x[y, c, ex] = g_ref[c * chunk : (c + 1) * chunk]
    make_rows(y)
    make_signs(0, y)
    make_signs(1, y)
    key_copy.wait_recv()
    make_rows(other_y)
    make_signs(0, other_y)
    for c in range(NC):
        c_copies[c].wait_recv()
    multiply_own(0)
    forward(0)
    make_signs(1, other_y)
    multiply_own(1)
    f_copies[0].wait_recv()
    multiply(0, 1, 0)
    multiply(0, 1, 1)
    forward(1)
    make_signs(2, y)
    f_copies[1].wait_recv()
    multiply(1, 1, 0)
    multiply(1, 1, 1)
    finish(0, 0)
    finish(0, 1)
    forward(2)
    make_signs(2, other_y)
    f_copies[2].wait_recv()
    multiply(2, 1, 0)
    multiply(2, 1, 1)
    finish(1, 0)
    finish(1, 1)
    forward(3)
    multiply_own(2)
    f_copies[3].wait_recv()
    multiply(3, 1, 0)
    multiply(3, 1, 1)
    finish(2, 0)
    finish(2, 1)
    multiply(0, 2, 2)
    multiply(2, 2, 2)
    finish(0, 2)
    finish(3, 0)
    finish(3, 1)
    finish(1, 2)
    make_signs(3, y)
    make_signs(3, other_y)
    finish(2, 2)
    multiply_own(3)
    multiply(0, NC, 3)
    settle(0)
    settle(1)
    finish(3, 2)
    settle(2)
    settle(3)

    whole = feats[...].reshape(2 * ex_rows, width)
    product = lax.dot_general(
        whole, whole, (((1,), (1,)), ((), ())), preferred_element_type=jnp.float32
    ) * (1.0 / math.sqrt(K))
    for half in range(2):
        columns = product[:, half * 128 : (half + 1) * 128].astype(jnp.bfloat16)
        kout[half] = columns.reshape(8, 32, 128)

    def k_copy(k):
        target = lax.rem(me + k, 16)
        return remote(
            kout.at[target % 2, target // 2], kin.at[k], k_send.at[k], k_recv.at[k], at_offset(k)
        )

    for k in range(1, 16):
        k_copy(k).start()
    feat_ref[:, pl.ds(pl.multiple_of(ex * width, width), width)] = feats[ex]
    for c in range(NC):
        fx_copy(c).wait_recv()
    feat_ref[:, pl.ds(pl.multiple_of(other_ex * width, width), width)] = feats_in[...]
    total = kout[ex, par].astype(jnp.float32)
    for k in range(1, 16):
        k_copy(k).wait_recv()
        total += kin[k].astype(jnp.float32)
    kern_ref[...] = total

    key_copy.wait_send()
    for c in range(NC):
        y_copies[c].wait_send()
        c_copies[c].wait_send()
        f_copies[c].wait_send()
        fx_copy(c).wait_send()
        for s in range(3):
            end_copy(c, s).wait_send()
    for k in range(1, 16):
        k_copy(k).wait_send()


def write_kernel(feat_in, kern_in, feat_ref, kern_ref):
    feat_ref[...] = feat_in[...]
    kern_ref[...] = kern_in[...]


def line(gradients, proj_seed, block_keys):
    ex_rows, params = gradients.shape
    chunk = ex_rows // NC
    width = K // 16
    dma = pltpu.SemaphoreType.DMA
    bf16 = jnp.bfloat16
    pair = pl.pallas_call(
        line_kernel,
        out_shape=(
            jax.ShapeDtypeStruct((ex_rows, K // 8), bf16),
            jax.ShapeDtypeStruct((2 * ex_rows // 8, ex_rows), jnp.float32),
        ),
        in_specs=[
            pl.BlockSpec(memory_space=pltpu.SMEM),
            pl.BlockSpec(memory_space=pltpu.SMEM),
            pl.BlockSpec(memory_space=pltpu.VMEM),
        ],
        out_specs=(
            pl.BlockSpec(memory_space=pltpu.VMEM),
            pl.BlockSpec(memory_space=pltpu.VMEM),
        ),
        scratch_shapes=[
            pltpu.VMEM((2, NC, 2, chunk, params), bf16),
            pltpu.VMEM((STEPS, 2, params, width), bf16),
            pltpu.VMEM((2, params, 128), jnp.int32),
            pltpu.VMEM((2, 8, 128), jnp.int32),
            pltpu.VMEM((STEPS, NC, 2 * chunk, width), jnp.float32),
            pltpu.VMEM((NC, 3, 2 * chunk, width), bf16),
            pltpu.VMEM((6, NC, 2 * chunk, width), bf16),
            pltpu.VMEM((2, ex_rows, width), bf16),
            pltpu.VMEM((ex_rows, width), bf16),
            pltpu.VMEM((2, 8, 32, 128), bf16),
            pltpu.VMEM((16, 32, 128), bf16),
            dma((NC,)), dma((NC,)), dma((NC,)), dma((NC,)), dma((NC,)), dma((NC,)),
            dma((2,)),
            dma((NC, 3)), dma((6, NC)), dma((NC,)), dma((NC,)), dma((16,)), dma((16,)),
        ],
        compiler_params=pltpu.CompilerParams(
            collective_id=0, has_side_effects=True, vmem_limit_bytes=56 * 1024 * 1024
        ),
    )(proj_seed, block_keys, gradients)
    return pl.pallas_call(
        write_kernel,
        out_shape=tuple(jax.ShapeDtypeStruct(part.shape, part.dtype) for part in pair),
    )(*pair)


def solution(mesh):
    placed = (P(("grp", "ex"), "par"), P(), P(None, "par"))
    special = mesh.shape["par"] == 8 and mesh.shape["ex"] == 2
    return jax.shard_map(
        line if special else general,
        mesh=mesh,
        in_specs=placed,
        out_specs=(P(("grp", "ex"), "par"), P(("grp", "par"), "ex")),
        check_vma=False,
    )
```
